32 devices in a mesh: grp: 2 (over core), dp: 4 (over y, x), sp: 4 (over z).
Axes of the slice: x: 2, y: 2, z: 4, core: 2. Of those that a mesh axis runs over, the one named last changes fastest.
Arguments:
- vis: bfloat16 [512, 5120], P(('grp', 'dp', 'sp')), may hold values from -6 to 6
- merge_weight: bfloat16 [5120, 8192], P('dp', ('grp', 'sp')), may hold values from -0.078125 to 0.078125
- img_counts: int32 [32], P('dp'), may hold values from 1 to 16
- img_pos: int32 [512], P(('grp', 'dp', 'sp')), may hold values from 0 to 127, as said below
- text: bfloat16 [4096, 8192], P(('grp', 'dp', 'sp')), may hold values from -6 to 6
- cot: bfloat16 [4096, 8192], P(('grp', 'dp', 'sp')), may hold values from -6 to 6
- gain: float32 [8192], replicated, may hold values from 0.25 to 1.75
Outputs:
- vis_grad: bfloat16 [512, 5120], P(('grp', 'dp', 'sp'))
- gain_grad: float32 [8192], replicated
The draws below stay inside these ranges and needn't reach their ends.
Inputs may be any that keep to these rules, and one draw needn't show every extreme that they name: `img_pos`: within one device's block the 16 positions are distinct. `img_counts`: the counts of one image group sum to at most 128.
All inputs are finite; a program needn't handle non-finite values.
Results may differ from the reference program's by a relative error of at most 0.014.
Values may be sent and summed in bfloat16 or wider, within the bound.
No kernel may reach another device: no remote copies, remote signals or barrier semaphores. Data moves between devices by JAX's collectives and lax.ppermute only.
A program may use at most 128 MiB of HBM per device.

```python
import jax
import jax.numpy as jnp
from jax import lax

DM = 8192
D_MERGE = 5120
RB = 16
TOK_DEV = 128
IMG_D = 8
VT_D = 128
VIS_ROWS = 512
TOKENS = 4096
IMAGES = 32
N_GRP = 2
N_DP = 4
N_SP = 4


def draw_img_pos(key, part):
    blocks = VIS_ROWS // RB

    def one_block(index):
        order = jax.random.permutation(jax.random.fold_in(key, index), TOK_DEV)
        return order[:RB].astype(jnp.int32)
    return jax.vmap(one_block)(jnp.arange(blocks, dtype=jnp.int32)).reshape(VIS_ROWS)


def with_ends(result, key, smallest, largest):
    extent = result.shape
    index_at = [jax.random.randint(jax.random.fold_in(key, axis), (), 0, extent[axis]) for axis in range(len(extent))]
    result = result.at[tuple(index_at)].set(smallest)
    longest = extent.index(max(extent))
    index_at[longest] = (index_at[longest] + 1) % extent[longest]
    return result.at[tuple(index_at)].set(largest)


def steps_of(stream_key, extent, cuts, least, top_value):
    level = 1.0
    for dim, parts in cuts:
        steps = jax.random.uniform(jax.random.fold_in(jax.random.fold_in(stream_key, 6), dim), (parts,), jnp.float32, least / len(cuts), top_value / len(cuts))
        level = level * jnp.repeat(jnp.exp(steps), extent[dim] // parts).reshape((-1,) + (1,) * (len(extent) - 1 - dim))
    return level


def normal_values(own_key, extent, spread, limit, split=(), kind=jnp.bfloat16):
    values = jax.random.normal(own_key, extent, jnp.float32) * spread
    if len(split) > 0:
        values = steps_of(own_key, extent, split, -0.22, 0.18) * values
    return jnp.clip(values, min=-limit, max=limit).astype(kind)


def setup_inputs(seed: int = 0) -> dict:
    splits = jax.random.split(jax.random.key(seed), 8)
    vis = normal_values(splits[0], (VIS_ROWS, D_MERGE), 1.0, 6.0, ((0, 32),))
    merge_weight = normal_values(splits[1], (D_MERGE, DM), D_MERGE ** -0.5, 0.078125, ((0, 4), (1, 8)))
    img_counts = with_ends(jax.random.randint(splits[2], (IMAGES,), 1, VT_D // IMG_D + 1), jax.random.fold_in(splits[2], 1), 1, (VT_D // IMG_D + 1) - 1).astype(jnp.int32)
    img_pos = draw_img_pos(jax.random.fold_in(splits[7], 71), 0)
    text = normal_values(splits[4], (TOKENS, DM), 1.0, 6.0, ((0, 32),))
    cot = normal_values(splits[5], (TOKENS, DM), 1.0, 6.0, ((0, 32),))
    gain = jnp.clip(1.0 + 0.15 * jax.random.normal(splits[6], (DM,), jnp.float32), 0.25, 1.75)
    return dict(vis=vis, merge_weight=merge_weight, img_counts=img_counts, img_pos=img_pos, text=text, cot=cot, gain=gain)


def one_block(vis_b, pos_b, text_b, cot_b, live_b, merge_weight, gain):
    emb = jnp.dot(vis_b, merge_weight, preferred_element_type=jnp.float32).astype(jnp.bfloat16)
    places = jnp.arange(TOK_DEV, dtype=jnp.int32)
    select = (pos_b[None, :] == places[:, None]) & (live_b[None, :] > 0)
    taken = jnp.any(select, axis=1)
    placed = jnp.dot(select.astype(jnp.bfloat16), emb, preferred_element_type=jnp.float32)
    hidden = jnp.where(taken[:, None], placed, text_b.astype(jnp.float32))
    rinv = lax.rsqrt(lax.optimization_barrier(jnp.mean(hidden * hidden, axis=1, keepdims=True)) + 1e-06)
    cotf = cot_b.astype(jnp.float32)
    part_gain = lax.optimization_barrier(jnp.sum(cotf * hidden * rinv, axis=0))
    scaled = cotf * gain[None, :]
    inner = lax.optimization_barrier(jnp.mean(scaled * hidden, axis=1, keepdims=True))
    dhid = (rinv * scaled - hidden * rinv ** 3 * inner).astype(jnp.bfloat16)
    demb = jnp.dot(select.astype(jnp.bfloat16).T, dhid, preferred_element_type=jnp.float32)
    demb = jnp.where(live_b[:, None] > 0, demb, 0.0).astype(jnp.bfloat16)
    slices = N_GRP * N_SP
    width = DM // slices
    demb_s = demb.astype(jnp.float32).reshape(RB, slices, width)
    weight_s = merge_weight.astype(jnp.float32).reshape(D_MERGE, slices, width)
    partials = jnp.einsum('rkf,dkf->krd', demb_s, weight_s).astype(jnp.bfloat16)
    grad = lax.optimization_barrier(jnp.sum(partials.astype(jnp.float32), axis=0))
    return (grad.astype(jnp.bfloat16), part_gain)

def reference(vis, merge_weight, img_counts, img_pos, text, cot, gain):
    blocks = VIS_ROWS // RB
    totals = lax.optimization_barrier(jnp.sum(img_counts.reshape(N_DP, IMG_D), axis=1)).astype(jnp.int32)
    index = jnp.arange(blocks, dtype=jnp.int32)
    grp_of = index // (N_DP * N_SP)
    dp_of = index // N_SP % N_DP
    sp_of = index % N_SP
    first = (grp_of * N_SP + sp_of) * RB
    rows = first[:, None] + jnp.arange(RB, dtype=jnp.int32)[None, :]
    live = (rows < totals[dp_of][:, None]).astype(jnp.int32)

    def step(items):
        vis_b, pos_b, text_b, cot_b, live_b = items
        return one_block(vis_b, pos_b, text_b, cot_b, live_b, merge_weight, gain)
    grads, gains = lax.map(step, (vis.reshape(blocks, RB, D_MERGE), img_pos.reshape(blocks, RB), text.reshape(blocks, TOK_DEV, DM), cot.reshape(blocks, TOK_DEV, DM), live))
    return (grads.reshape(VIS_ROWS, D_MERGE), lax.optimization_barrier(jnp.sum(gains, axis=0)))
```

```python
import jax
import jax.numpy as jnp
from jax import lax
from jax.sharding import PartitionSpec as P

F32 = jnp.float32
BF16 = jnp.bfloat16
DIRECT = 8


def pairs(n, k):
    return [(i, i ^ k) for i in range(n)]


def relative(x, me):
    n = x.shape[0]
    return jnp.stack([lax.dynamic_index_in_dim(x, me ^ k, 0, keepdims=False) for k in range(n)])


def swap(blocks, axis):
    n = len(blocks)
    if n <= DIRECT:
        return [blocks[0]] + [lax.ppermute(blocks[k], axis, pairs(n, k)) for k in range(1, n)]
    me = lax.axis_index(axis)
    index = me ^ jnp.arange(n)
    sent = jnp.take(jnp.stack(blocks), index, axis=0)
    got = lax.all_to_all(sent, axis, 0, 0, tiled=True)
    got = jnp.take(got, index, axis=0)
    return [got[k] for k in range(n)]


def share(x, axis):
    n = lax.axis_size(axis)
    if n <= DIRECT:
        return [x] + [lax.ppermute(x, axis, pairs(n, k)) for k in range(1, n)]
    me = lax.axis_index(axis)
    got = jnp.take(lax.all_gather(x, axis), me ^ jnp.arange(n), axis=0)
    return [got[k] for k in range(n)]


def body(vis, weight, img_counts, img_pos, text, cot, gain):
    n_g, n_d, n_s = (lax.axis_size(a) for a in ("grp", "dp", "sp"))
    g, d, s = (lax.axis_index(a) for a in ("grp", "dp", "sp"))
    rb = vis.shape[0]
    toks, dm = text.shape
    dc, kc = weight.shape
    rows = n_g * n_s * rb

    own = relative(vis.reshape(rb, n_d, dc).transpose(1, 0, 2), d)
    mine = jnp.stack(swap([own[k] for k in range(n_d)], "dp"))
    along = share(mine, "sp")
    pieces = [share(p, "grp") for p in along]
    every = jnp.stack([jnp.stack([pieces[j][i] for j in range(n_s)]) for i in range(n_g)])
    every = every.transpose(2, 0, 1, 3, 4).reshape(n_d, rows, dc)
    part = [jnp.dot(every[k], weight, preferred_element_type=F32).astype(BF16) for k in range(n_d)]
    got = swap(part, "dp")
    emb = sum(p.astype(F32) for p in got).astype(BF16).astype(F32)

    total = jnp.sum(img_counts)
    group_row = (g * n_s + s) * rb + jnp.arange(rb, dtype=jnp.int32)
    live = group_row < total
    places = jnp.arange(toks, dtype=jnp.int32)
    select = (img_pos[None, :] == places[:, None]) & live[None, :]
    taken = jnp.any(select, axis=1)
    picked = jnp.dot(select.astype(BF16).T, cot, preferred_element_type=F32).astype(BF16)
    picked = picked.reshape(rb, n_g, n_s, kc).transpose(2, 1, 0, 3)
    picked = relative(picked, s)
    seen = swap([picked[k] for k in range(n_s)], "sp")
    seen = relative(jnp.stack(seen, axis=1), g)
    seen = jnp.stack(swap([seen[k] for k in range(n_g)], "grp"))
    cotf = seen.reshape(rows, kc).astype(F32)

    textf = text.astype(F32)
    keep = jnp.where(taken[:, None], 0.0, lax.rsqrt(jnp.mean(textf * textf, axis=1, keepdims=True) + 1e-06))
    text_gain = jnp.sum(cot.astype(F32) * textf * keep, axis=0)
    text_gain = relative(text_gain.reshape(n_g, n_s, kc), g)
    text_gain = relative(text_gain.transpose(1, 0, 2), s)

    gk = lax.dynamic_slice_in_dim(gain, (g * n_s + s) * kc, kc)
    scaled = cotf * gk[None, :]
    stats = jnp.stack([jnp.sum(emb * emb, axis=1), jnp.sum(scaled * emb, axis=1)])
    n_stat = 2 * rows
    near = jnp.concatenate([stats.reshape(-1), text_gain[:, 1].reshape(-1)])
    far = lax.ppermute(near, "grp", pairs(n_g, 1))
    far_stats = far[:n_stat].reshape(2, n_g, n_s, rb)[:, ::-1]
    stats = stats.reshape(2, n_g, n_s, rb) + far_stats
    text_gain = text_gain[:, 0] + far[n_stat:].reshape(n_s, kc)
    sent = [jnp.concatenate([stats.reshape(-1), text_gain[k]]) for k in range(n_s)]
    got = swap(sent, "sp")
    stats = sum(
        got[k][:n_stat].reshape(2, n_g, n_s, rb)[:, :, jnp.array([j ^ k for j in range(n_s)])] for k in range(n_s)
    )
    text_gain = sum(got[k][n_stat:] for k in range(n_s))
    stats = stats.reshape(2, rows, 1) / dm
    rinv = lax.rsqrt(stats[0] + 1e-06)
    inner = stats[1]

    row = (
        ((g ^ jnp.arange(n_g))[:, None, None] * n_s + (s ^ jnp.arange(n_s))[None, :, None]) * rb
        + jnp.arange(rb)[None, None, :]
    ).reshape(rows, 1)
    alive = row < total
    demb = jnp.where(alive, rinv * scaled - emb * rinv**3 * inner, 0.0).astype(BF16)
    gain_part = text_gain + jnp.sum(jnp.where(alive, cotf * emb * rinv, 0.0), axis=0)

    rows_k = share(demb, "dp")
    gain_k = sum(share(gain_part, "dp"))
    back = jnp.stack(
        [
            lax.dot_general(r, weight, (((1,), (1,)), ((), ())), preferred_element_type=F32).astype(BF16)
            for r in rows_k
        ]
    ).reshape(n_d, n_g, n_s, rb, dc)
    got = lax.ppermute(back[:, 1], "grp", pairs(n_g, 1))
    half = (back[:, 0].astype(F32) + got.astype(F32)).astype(BF16)
    got = swap([half[:, k] for k in range(n_s)], "sp")
    done = sum(x.astype(F32) for x in got).astype(BF16)
    got = relative(jnp.stack(swap([done[k] for k in range(n_d)], "dp")), d)
    vis_grad = got.transpose(1, 0, 2).reshape(rb, n_d * dc)

    gains = relative(jnp.stack(share(gain_k, "sp")), s)
    gains = relative(jnp.stack(share(gains, "grp")), g)
    return vis_grad, gains.reshape(dm)


def solution(mesh):
    return jax.shard_map(
        body,
        mesh=mesh,
        in_specs=(
            P(("grp", "dp", "sp"), None),
            P("dp", ("grp", "sp")),
            P("dp"),
            P(("grp", "dp", "sp")),
            P(("grp", "dp", "sp"), None),
            P(("grp", "dp", "sp"), None),
            P(),
        ),
        out_specs=(P(("grp", "dp", "sp"), None), P()),
        check_vma=False,
    )
```
